32 devices in a mesh: groups: 2 (over y), tok: 4 (over z), head: 4 (over x, core).
Axes of the slice: x: 2, y: 2, z: 4, core: 2. Of those that a mesh axis runs over, the one named last changes fastest.
Arguments:
- hidden: bfloat16 [2560, 8192], P(('groups', 'tok'), 'head'), parts along dimension 0, may hold values from -6 to 6
- positions: int32 [2560], P(('groups', 'tok')), parts along dimension 0, may hold values from 0 to 1279, as said below
- norm_gain: float32 [8192], P('head'), may hold values from 0.1 to 1.9
- w_key: bfloat16 [8192, 1024], P('head'), may hold values from -0.0625 to 0.0625
- w_value: bfloat16 [8192, 1024], P('head'), may hold values from -0.0625 to 0.0625
- queries: bfloat16 [512, 8192], P(('groups', 'tok'), 'head'), parts along dimension 0, may hold values from -400 to 400
- lengths: int32 [512], P(('groups', 'tok')), parts along dimension 0, may hold values from 1 to 1280
Outputs:
- attended: bfloat16 [512, 8192], P(('groups', 'tok'), 'head'), parts along dimension 0
The draws below stay inside these ranges and needn't reach their ends.
There are 2 independent parts, one for each index of `groups`. The reference program is written for one: setup_inputs(seed, part) draws one part's arguments, and reference() takes and returns one part's arrays. A program takes and returns all parts, laid end to end along the dimension named above; an argument that names none is the same for every part. Nothing has to cross between parts.
Inputs may be any that keep to these rules, and one draw needn't show every extreme that they name: `positions`: each of 0 to 1279 appears once.
All inputs are finite; a program needn't handle non-finite values.
Results may differ from the reference program's by a relative error of at most 0.025.
The reference program's roundings to bfloat16 on the way (of `normed`, `keys`, `values` and `weights`) count: a program that leaves them out, or rounds other values in their place, can miss the bound.
Values may be sent and summed in bfloat16 or wider, within the bound.
A program may use at most 64 MiB of HBM per device.

```python
import jax
import jax.numpy as jnp
from jax import lax

D = 8192
KVH = 8
HD = 128
QPK = 8
ROWS = 256
QH = 64
PREFIX = 1280


def draw_positions(key, part):
    pages = PREFIX // 8
    order = jax.random.permutation(jax.random.fold_in(key, 11), pages).astype(jnp.int32)
    index = jnp.arange(PREFIX, dtype=jnp.int32)
    return order[index // 8] * 8 + index % 8


def draw_queries(key, part):
    base = jax.random.truncated_normal(jax.random.fold_in(key, 23), -6.0, 6.0, (ROWS, QH * HD), jnp.float32)
    return base.astype(jnp.bfloat16)


def plant(drawn, rng, least, top_value):
    dims = drawn.shape
    index_at = [jax.random.randint(jax.random.fold_in(rng, axis), (), 0, dims[axis]) for axis in range(len(dims))]
    drawn = drawn.at[tuple(index_at)].set(least)
    longest = dims.index(max(dims))
    index_at[longest] = (index_at[longest] + 1) % dims[longest]
    return drawn.at[tuple(index_at)].set(top_value)


def shard_levels(key, dims, shards, low, high):
    factor_of, own = 1.0, jax.random.fold_in(key, 6)
    for position, shards_of in shards:
        heights = jnp.exp(jax.random.uniform(jax.random.fold_in(own, position), (shards_of,), jnp.float32, low / len(shards), high / len(shards)))
        factor_of = factor_of * jnp.repeat(heights, dims[position] // shards_of).reshape([-1 if axis == position else 1 for axis in range(len(dims))])
    return factor_of


def normal_values(rng, dims, spread, most, pieces=(), kind=jnp.bfloat16):
    level = shard_levels(rng, dims, pieces, -0.22, 0.18) if pieces else 1.0
    drawn = jax.random.normal(rng, dims, jnp.float32) * spread * level
    return jnp.minimum(jnp.maximum(drawn, -most), most).astype(kind)


def setup_inputs(seed: int = 0, part: int = 0) -> dict:
    splits = jax.random.split(jax.random.key(seed), 8)
    own_keys = jax.random.split(jax.random.fold_in(splits[7], part), 8)
    return {
        "hidden": normal_values(own_keys[0], (PREFIX, D), 1.0, 6.0, ((0, 4), (1, 4))),
        "positions": draw_positions(jax.random.fold_in(jax.random.fold_in(splits[7], part), 71), part),
        "norm_gain": jnp.clip(1.0 + 0.18 * jax.random.normal(splits[2], (D,), jnp.float32), 0.1, 1.9),
        "w_key": normal_values(splits[3], (D, KVH * HD), D ** -0.5, 0.0625, ((0, 4),)),
        "w_value": normal_values(splits[4], (D, KVH * HD), D ** -0.5, 0.0625, ((0, 4),)),
        "queries": draw_queries(jax.random.fold_in(jax.random.fold_in(splits[7], part), 71), part),
        "lengths": plant(jax.random.randint(own_keys[6], (ROWS,), 1, PREFIX + 1), jax.random.fold_in(own_keys[6], 1), 1, PREFIX).astype(jnp.int32),
    }


def rotate_keys(keys, positions):
    half = HD // 2
    freq = 500000.0 ** (-(jnp.arange(half, dtype=jnp.float32) * 2.0) / HD)
    angle = positions.astype(jnp.float32)[:, None] * freq[None, :]
    cosine = jnp.cos(angle)[:, None, :]
    sine = jnp.sin(angle)[:, None, :]
    first = keys[..., :half]
    second = keys[..., half:]
    return jnp.concatenate([first * cosine - second * sine, second * cosine + first * sine], axis=-1)

def reference(hidden, positions, norm_gain, w_key, w_value, queries, lengths):
    wide = hidden.astype(jnp.float32)
    meansq = lax.optimization_barrier(jnp.mean(wide * wide, axis=1, keepdims=True))
    normed = (wide * lax.rsqrt(meansq + 1e-05) * norm_gain).astype(jnp.bfloat16)
    key_raw = jnp.dot(normed, w_key, preferred_element_type=jnp.float32).reshape(PREFIX, KVH, HD)
    keys = rotate_keys(key_raw, positions).astype(jnp.bfloat16)
    values = jnp.dot(normed, w_value, preferred_element_type=jnp.float32).astype(jnp.bfloat16).reshape(PREFIX, KVH, HD)
    valid = positions[None, :] < lengths[:, None]
    grouped = queries.reshape(ROWS, KVH, QPK, HD)
    scale = HD ** (-0.5)

    def one_head(index):
        query_head = grouped[:, index]
        key_head = keys[:, index]
        value_head = values[:, index]
        scores = jnp.einsum('rgd,pd->rgp', query_head.astype(jnp.float32), key_head.astype(jnp.float32)) * scale
        scores = jnp.where(valid[:, None, :], scores, -1e+30)
        top = lax.optimization_barrier(jnp.max(scores, axis=2, keepdims=True))
        weights = jnp.exp(scores - top).astype(jnp.bfloat16)
        numer = jnp.einsum('rgp,pd->rgd', weights.astype(jnp.float32), value_head.astype(jnp.float32))
        denom = lax.optimization_barrier(jnp.sum(weights.astype(jnp.float32), axis=2, keepdims=True))
        return numer / denom
    result = lax.map(one_head, jnp.arange(KVH, dtype=jnp.int32))
    return result.transpose(1, 0, 2, 3).reshape(ROWS, QH * HD).astype(jnp.bfloat16)
```

```python
import functools

import jax
import jax.numpy as jnp
from jax import lax
from jax.experimental import pallas as pl
from jax.experimental.pallas import tpu as pltpu
from jax.sharding import PartitionSpec as P

HD = 128
QPK = 8
THETA = 500000.0
EPS = 1e-05
W_PARTS = 4
TOK_SPLIT = 2
WIRE = jnp.bfloat16
MESH = pl.DeviceIdType.MESH


def kernel(
    T, H, full_width,
    hidden_hbm, pos_ref, gain_ref, wk_hbm, wv_hbm, q_hbm, len_ref,
    out_ref,
    hid, normed, wbuf, qbuf, squares, cos_buf, sin_buf, pos_all, mask_len,
    pair_send, pair_recv, keep, x_send, x_recv, kv, scores, top_lanes, numer, denom,
    load_sem, sq_send, sq_recv, pos_send, pos_recv,
    pair_ssem, pair_rsem, x_ssem, x_rsem, z_ssem, z_rsem,
):
    X = H // 2
    n_tok, width = hid.shape
    kw = kv.shape[-1]
    kv_here = kw // HD
    rows = qbuf.shape[0]
    nt = n_tok // TOK_SPLIT
    t = lax.axis_index("tok")
    head = lax.axis_index("head")
    xi, core = head // 2, lax.rem(head, 2)
    partner = xi * 2 + (1 - core)

    loads = [pltpu.make_async_copy(hidden_hbm, hid, load_sem.at[0])]
    w_loads = []
    part = width // W_PARTS
    for which, src in enumerate((wk_hbm, wv_hbm)):
        group = []
        for i in range(W_PARTS):
            group.append(
                pltpu.make_async_copy(
                    src.at[pl.ds(i * part, part)],
                    wbuf.at[which, pl.ds(i * part, part)],
                    load_sem.at[2 + which * W_PARTS + i],
                )
            )
        w_loads.append(group)
    q_load = pltpu.make_async_copy(q_hbm, qbuf, load_sem.at[1])
    loads[0].start()
    for group in w_loads:
        for c in group:
            c.start()
    q_load.start()

    barrier = pltpu.get_barrier_semaphore()
    for d in range(1, H):
        pl.semaphore_signal(
            barrier, inc=1, device_id={"head": lax.rem(head + d, H)}, device_id_type=MESH
        )
    for d in range(1, T):
        pl.semaphore_signal(
            barrier, inc=1, device_id={"tok": lax.rem(t + d, T)}, device_id_type=MESH
        )

    loads[0].wait()
    acc = jnp.zeros((n_tok, HD), jnp.float32)
    for i in range(width // HD):
        piece = hid[:, i * HD:(i + 1) * HD].astype(jnp.float32)
        acc = acc + piece * piece
    local = jnp.sum(acc.T, axis=0, keepdims=True)
    squares[pl.ds(head, 1)] = jnp.broadcast_to(local, (8, n_tok))[None]

    pl.semaphore_wait(barrier, H - 1 + T - 1)
    sq_copies = []
    for d in range(1, H):
        c = pltpu.make_async_remote_copy(
            src_ref=squares.at[head], dst_ref=squares.at[head],
            send_sem=sq_send.at[d], recv_sem=sq_recv.at[d],
            device_id={"head": lax.rem(head + d, H)}, device_id_type=MESH,
        )
        c.start()
        sq_copies.append(c)
    pos_copies = []
    for d in range(1, T):
        c = pltpu.make_async_remote_copy(
            src_ref=pos_ref, dst_ref=pos_all.at[t],
            send_sem=pos_send.at[d], recv_sem=pos_recv.at[d],
            device_id={"tok": lax.rem(t + d, T)}, device_id_type=MESH,
        )
        c.start()
        pos_copies.append(c)
    pos_all[pl.ds(t, 1)] = pos_ref[...][None]

    pos_col = jnp.broadcast_to(pos_ref[...].astype(jnp.float32), (HD, n_tok)).T
    lane = lax.broadcasted_iota(jnp.int32, (1, HD), 1)
    half = HD // 2
    idx = jnp.where(lane < half, lane, lane - half).astype(jnp.float32)
    freq = THETA ** (-(idx * 2.0) / HD)
    angle = pos_col * freq
    cos_buf[...] = jnp.cos(angle)
    sine = jnp.sin(angle)
    sin_buf[...] = jnp.where(lane < half, -sine, sine)
    mask_len[...] = jnp.broadcast_to(len_ref[...].astype(jnp.float32), (HD, rows)).T.astype(jnp.int32)

    for c in sq_copies:
        c.wait()
    total = squares[0]
    for i in range(1, H):
        total = total + squares[i]
    r = lax.rsqrt(total[0:1] / full_width + EPS)
    r_col = jnp.broadcast_to(r, (HD, n_tok)).T
    for i in range(width // HD):
        cols = slice(i * HD, (i + 1) * HD)
        wide = hid[:, cols].astype(jnp.float32)
        normed[:, cols] = (wide * r_col * gain_ref[:, cols]).astype(jnp.bfloat16)

    units = [(which, th) for which in range(2) for th in range(TOK_SPLIT)]

    def project(which, th, block):
        cols = pl.ds(pl.multiple_of(block * kw, kw), kw)
        return jnp.dot(
            normed[th * nt:(th + 1) * nt, :], wbuf[which, :, cols],
            preferred_element_type=jnp.float32,
        )

    def pair_copy(u, dx):
        return pltpu.make_async_remote_copy(
            src_ref=pair_send.at[u, dx], dst_ref=pair_recv.at[u, dx],
            send_sem=pair_ssem.at[u, dx], recv_sem=pair_rsem.at[u, dx],
            device_id={"head": partner}, device_id_type=MESH,
        )

    def x_copy(u, dx):
        return pltpu.make_async_remote_copy(
            src_ref=x_send.at[u, dx - 1], dst_ref=x_recv.at[u, dx - 1],
            send_sem=x_ssem.at[u, dx - 1], recv_sem=x_rsem.at[u, dx - 1],
            device_id={"head": lax.rem(xi + dx, X) * 2 + core}, device_id_type=MESH,
        )

    def kv_at(u, block):
        which, th = units[u]
        return kv.at[block, which, pl.ds(th * nt, nt)]

    def z_copy(u, direction, step, block):
        to = lax.rem(t + 1, T) if direction == 0 else lax.rem(t + T - 1, T)
        return pltpu.make_async_remote_copy(
            src_ref=kv_at(u, block), dst_ref=kv_at(u, block),
            send_sem=z_ssem.at[direction, step, u], recv_sem=z_rsem.at[direction, step, u],
            device_id={"tok": to}, device_id_type=MESH,
        )

    def can_send(direction, step):
        if direction == 0:
            return jnp.logical_and(t + 1 < T, t - step >= 0)
        return jnp.logical_and(t - 1 >= 0, t + step < T)

    def can_recv(direction, step):
        if direction == 0:
            return t - 1 - step >= 0
        return t + 1 + step < T

    def arriving(direction, step):
        block = t - 1 - step if direction == 0 else t + 1 + step
        return jnp.clip(block, 0, T - 1)

    def leaving(direction, step):
        block = t - step if direction == 0 else t + step
        return jnp.clip(block, 0, T - 1)

    def stage_matmul(u):
        which, th = units[u]
        for dx in list(range(1, X)) + [0]:
            to = lax.rem(xi + dx, X)
            pair_send[u, dx] = project(which, th, to * 2 + (1 - core))
            pair_copy(u, dx).start()
            keep[u, dx] = project(which, th, to * 2 + core)

    def stage_chip(u):
        for dx in range(1, X):
            pair_copy(u, dx).wait_recv()
            x_send[u, dx - 1] = (keep[u, dx] + pair_recv[u, dx]).astype(WIRE)
            x_copy(u, dx).start()

    def stage_finish(u):
        which, th = units[u]
        pair_copy(u, 0).wait_recv()
        whole = keep[u, 0] + pair_recv[u, 0]
        for dx in range(1, X):
            x_copy(u, dx).wait_recv()
            whole = whole + x_recv[u, dx - 1].astype(jnp.float32)
        if which == 0:
            cosine = cos_buf[th * nt:(th + 1) * nt]
            sine = sin_buf[th * nt:(th + 1) * nt]
            pieces = []
            for j in range(kv_here):
                k = whole[:, j * HD:(j + 1) * HD]
                pieces.append(k * cosine + pltpu.roll(k, half, 1) * sine)
            whole = jnp.concatenate(pieces, axis=1) if kv_here > 1 else pieces[0]
        kv[pl.ds(t, 1), which, th * nt:(th + 1) * nt] = whole.astype(jnp.bfloat16)[None]
        for direction in range(2):
            @pl.when(can_send(direction, 0))
            def _():
                z_copy(u, direction, 0, t).start()

    n_units = len(units)
    for u in range(n_units):
        which, th = units[u]
        if th == 0:
            for c in w_loads[which]:
                c.wait()
        stage_matmul(u)
        stage_chip(u)
        if u > 0:
            stage_finish(u - 1)
    stage_finish(n_units - 1)

    q_load.wait()
    for c in pos_copies:
        c.wait()

    top_lanes[...] = jnp.full(top_lanes.shape, -1e30, jnp.float32)
    scale = HD ** (-0.5)

    def score_block(block):
        valid = pos_all[block] < mask_len[:, :1]
        for j in range(kv_here):
            k = kv[block, 0, :, j * HD:(j + 1) * HD]
            for g in range(QPK):
                q = qbuf[:, (j * QPK + g) * HD:(j * QPK + g + 1) * HD]
                s = lax.dot_general(
                    q, k, (((1,), (1,)), ((), ())), preferred_element_type=jnp.float32
                ) * scale
                s = jnp.where(valid, s, -1e30)
                scores[block, j * QPK + g] = s
                top_lanes[j * QPK + g] = jnp.maximum(
                    top_lanes[j * QPK + g], jnp.max(s, axis=1, keepdims=True)
                )

    def value_block(block):
        for j in range(kv_here):
            v = kv[block, 1, :, j * HD:(j + 1) * HD]
            for g in range(QPK):
                e = j * QPK + g
                w = jnp.exp(scores[block, e] - top_lanes[e][:, :1]).astype(jnp.bfloat16)
                denom[e] += jnp.sum(w.astype(jnp.float32), axis=1, keepdims=True)
                numer[e] += jnp.dot(w, v, preferred_element_type=jnp.float32)

    numer[...] = jnp.zeros(numer.shape, jnp.float32)
    denom[...] = jnp.zeros(denom.shape, jnp.float32)
    score_block(t)
    k_units = [u for u in range(n_units) if units[u][0] == 0]
    v_units = [u for u in range(n_units) if units[u][0] == 1]

    def arrive(us, direction, step):
        for u in us:
            z_copy(u, direction, step, arriving(direction, step)).wait_recv()
            if step + 1 < T - 1:
                @pl.when(can_send(direction, step + 1))
                def _():
                    z_copy(u, direction, step + 1, leaving(direction, step + 1)).start()

    for step in range(T - 1):
        for us in (k_units, v_units):
            if us is v_units and step == T - 2:
                continue
            for direction in range(2):
                @pl.when(can_recv(direction, step))
                def _():
                    arrive(us, direction, step)
                    if us is k_units:
                        score_block(arriving(direction, step))
    value_block(t)
    for step in range(T - 1):
        for direction in range(2):
            @pl.when(can_recv(direction, step))
            def _():
                if step == T - 2:
                    arrive(v_units, direction, step)
                value_block(arriving(direction, step))
    for e in range(kv_here * QPK):
        out_ref[:, e * HD:(e + 1) * HD] = (numer[e] / denom[e]).astype(jnp.bfloat16)

    for u in range(n_units):
        for dx in range(X):
            pair_copy(u, dx).wait_send()
        for dx in range(1, X):
            x_copy(u, dx).wait_send()
        for step in range(T - 1):
            for direction in range(2):
                @pl.when(can_send(direction, step))
                def _():
                    z_copy(u, direction, step, leaving(direction, step)).wait_send()


def body(hidden, positions, norm_gain, w_key, w_value, queries, lengths):
    T, H = lax.axis_size("tok"), lax.axis_size("head")
    X = H // 2
    n_tok, width = hidden.shape
    rows, q_cols = queries.shape
    kw = w_key.shape[1] // H
    e = q_cols // HD
    nt = n_tok // TOK_SPLIT
    n_units = 2 * TOK_SPLIT
    f32, bf16 = jnp.float32, jnp.bfloat16
    vmem = pl.BlockSpec(memory_space=pltpu.VMEM)
    hbm = pl.BlockSpec(memory_space=pl.ANY)
    dma = pltpu.SemaphoreType.DMA
    scratch = [
        pltpu.VMEM((n_tok, width), bf16),
        pltpu.VMEM((n_tok, width), bf16),
        pltpu.VMEM((2, width, w_key.shape[1]), bf16),
        pltpu.VMEM((rows, q_cols), bf16),
        pltpu.VMEM((H, 8, n_tok), f32),
        pltpu.VMEM((n_tok, HD), f32),
        pltpu.VMEM((n_tok, HD), f32),
        pltpu.VMEM((T, 1, n_tok), jnp.int32),
        pltpu.VMEM((rows, HD), jnp.int32),
        pltpu.VMEM((n_units, X, nt, kw), f32),
        pltpu.VMEM((n_units, X, nt, kw), f32),
        pltpu.VMEM((n_units, X, nt, kw), f32),
        pltpu.VMEM((n_units, X - 1, nt, kw), WIRE),
        pltpu.VMEM((n_units, X - 1, nt, kw), WIRE),
        pltpu.VMEM((T, 2, n_tok, kw), bf16),
        pltpu.VMEM((T, e, rows, n_tok), f32),
        pltpu.VMEM((e, rows, HD), f32),
        pltpu.VMEM((e, rows, HD), f32),
        pltpu.VMEM((e, rows, HD), f32),
        dma((2 + 2 * W_PARTS,)),
        dma((H,)), dma((H,)),
        dma((T,)), dma((T,)),
        dma((n_units, X)), dma((n_units, X)),
        dma((n_units, X - 1)), dma((n_units, X - 1)),
        dma((2, T - 1, n_units)), dma((2, T - 1, n_units)),
    ]
    return pl.pallas_call(
        functools.partial(kernel, T, H, width * H),
        out_shape=jax.ShapeDtypeStruct((rows, q_cols), bf16),
        in_specs=[hbm, vmem, vmem, hbm, hbm, hbm, vmem],
        out_specs=vmem,
        scratch_shapes=scratch,
        compiler_params=pltpu.CompilerParams(
            collective_id=0, has_side_effects=True, vmem_limit_bytes=60 * 1024 * 1024
        ),
    )(
        hidden, positions.reshape(1, n_tok), norm_gain.reshape(1, width), w_key, w_value,
        queries, lengths.reshape(1, rows),
    )


def solution(mesh):
    in_specs = (
        P(("groups", "tok"), "head"),
        P(("groups", "tok")),
        P("head"),
        P("head", None),
        P("head", None),
        P(("groups", "tok"), "head"),
        P(("groups", "tok")),
    )
    out_specs = P(("groups", "tok"), "head")
    return jax.shard_map(body, mesh=mesh, in_specs=in_specs, out_specs=out_specs, check_vma=False)
```

```python
import functools

import jax
import jax.numpy as jnp
from jax import lax
from jax.experimental import pallas as pl
from jax.experimental.pallas import tpu as pltpu
from jax.sharding import PartitionSpec as P

HD = 128
QPK = 8
THETA = 500000.0
EPS = 1e-05
H_PARTS = 4
TOK_SPLIT = 2
WIRE = jnp.bfloat16
MESH = pl.DeviceIdType.MESH


def kernel(
    T, H, full_width,
    hidden_hbm, pos_ref, gain_ref, wk_hbm, wv_hbm, q_hbm, len_ref,
    out_ref,
    hid, normed, wbuf, qbuf, squares, cos_buf, sin_buf, pos_all, mask_len,
    pair_send, pair_recv, keep, x_send, x_recv, kv, scores, top_lanes, numer, denom,
    load_sem, sq_send, sq_recv, pos_send, pos_recv,
    pair_ssem, pair_rsem, x_ssem, x_rsem, z_ssem, z_rsem,
    q_extra, len_extra, mask_extra, far_out, far_stats, near_out, near_stats, off_ssem, off_rsem,
):
    X = H // 2
    n_tok, width = hid.shape
    kw = kv.shape[-1]
    kv_here = kv.shape[1]
    rows = qbuf.shape[0]
    nt = n_tok // TOK_SPLIT
    t = lax.axis_index("tok")
    head = lax.axis_index("head")
    xi, core = head // 2, lax.rem(head, 2)
    partner = xi * 2 + (1 - core)
    order = list(reversed(range(kv_here)))
    offload = kv_here > 1 and T >= 4
    moved = kv_here - 1 if offload else -1
    is_client = jnp.logical_or(t == 0, t == T - 1)
    is_helper = jnp.logical_or(t == 1, t == T - 2)
    other_end = jnp.where(t < T // 2, jnp.where(t == 0, 1, 0), jnp.where(t == T - 1, T - 2, T - 1))

    part = n_tok // H_PARTS
    h_loads = [
        pltpu.make_async_copy(
            hidden_hbm.at[pl.ds(i * part, part)], hid.at[pl.ds(i * part, part)], load_sem.at[1 + i]
        )
        for i in range(H_PARTS)
    ]
    w_loads = []
    at = 1 + H_PARTS
    for j in order:
        group = []
        for blk in range(H):
            for which, src in enumerate((wk_hbm, wv_hbm)):
                h = blk * kv_here + j
                group.append(
                    pltpu.make_async_copy(
                        src.at[:, pl.ds(h * HD, HD)],
                        wbuf.at[:, pl.ds(h * kw + which * HD, HD)],
                        load_sem.at[at],
                    )
                )
                at += 1
        w_loads.append(group)
    q_load = pltpu.make_async_copy(q_hbm, qbuf, load_sem.at[0])
    for c in h_loads:
        c.start()
    q_load.start()

    barrier = pltpu.get_barrier_semaphore()
    for d in range(1, H):
        pl.semaphore_signal(
            barrier, inc=1, device_id={"head": lax.rem(head + d, H)}, device_id_type=MESH
        )
    for d in range(1, T):
        pl.semaphore_signal(
            barrier, inc=1, device_id={"tok": lax.rem(t + d, T)}, device_id_type=MESH
        )

    sums = []
    for p in range(H_PARTS):
        h_loads[p].wait()
        acc = jnp.zeros((part, HD), jnp.float32)
        for i in range(width // HD):
            piece = hid[p * part:(p + 1) * part, i * HD:(i + 1) * HD].astype(jnp.float32)
            acc = acc + piece * piece
        sums.append(acc)
    for group in w_loads:
        for c in group:
            c.start()
    acc = jnp.concatenate(sums, axis=0)
    local = jnp.sum(acc.T, axis=0, keepdims=True)
    squares[pl.ds(head, 1)] = jnp.broadcast_to(local, (8, n_tok))[None]

    pl.semaphore_wait(barrier, H - 1 + T - 1)
    sq_copies = []
    for d in range(1, H):
        c = pltpu.make_async_remote_copy(
            src_ref=squares.at[head], dst_ref=squares.at[head],
            send_sem=sq_send.at[d], recv_sem=sq_recv.at[d],
            device_id={"head": lax.rem(head + d, H)}, device_id_type=MESH,
        )
        c.start()
        sq_copies.append(c)
    pos_copies = []
    for d in range(1, T):
        c = pltpu.make_async_remote_copy(
            src_ref=pos_ref, dst_ref=pos_all.at[t],
            send_sem=pos_send.at[d], recv_sem=pos_recv.at[d],
            device_id={"tok": lax.rem(t + d, T)}, device_id_type=MESH,
        )
        c.start()
        pos_copies.append(c)
    pos_all[pl.ds(t, 1)] = pos_ref[...][None]

    def off_copy(i, src, dst):
        return pltpu.make_async_remote_copy(
            src_ref=src, dst_ref=dst, send_sem=off_ssem.at[i], recv_sem=off_rsem.at[i],
            device_id={"tok": other_end}, device_id_type=MESH,
        )

    def ask_copies():
        cols = pl.ds(moved * QPK * HD, QPK * HD)
        return off_copy(0, qbuf.at[:, cols], q_extra), off_copy(1, len_ref, len_extra)

    def answer_copies():
        return off_copy(2, far_out, near_out), off_copy(3, far_stats, near_stats)

    q_load.wait()
    if offload:
        @pl.when(is_client)
        def _():
            for c in ask_copies():
                c.start()

    pos_col = jnp.broadcast_to(pos_ref[...].astype(jnp.float32), (HD, n_tok)).T
    lane = lax.broadcasted_iota(jnp.int32, (1, HD), 1)
    half = HD // 2
    idx = jnp.where(lane < half, lane, lane - half).astype(jnp.float32)
    freq = THETA ** (-(idx * 2.0) / HD)
    angle = pos_col * freq
    cos_buf[...] = jnp.cos(angle)
    sine = jnp.sin(angle)
    sin_buf[...] = jnp.where(lane < half, -sine, sine)
    mask_len[...] = jnp.broadcast_to(len_ref[...].astype(jnp.float32), (HD, rows)).T.astype(jnp.int32)

    for c in sq_copies:
        c.wait()
    total = squares[0]
    for i in range(1, H):
        total = total + squares[i]
    r = lax.rsqrt(total[0:1] / full_width + EPS)
    r_col = jnp.broadcast_to(r, (HD, n_tok)).T
    for i in range(width // HD):
        cols = slice(i * HD, (i + 1) * HD)
        wide = hid[:, cols].astype(jnp.float32)
        normed[:, cols] = (wide * r_col * gain_ref[:, cols]).astype(jnp.bfloat16)

    units = [(j, th) for j in order for th in range(TOK_SPLIT)]

    def project(j, th, block):
        cols = pl.ds(pl.multiple_of((block * kv_here + j) * kw, kw), kw)
        return jnp.dot(
            normed[th * nt:(th + 1) * nt, :], wbuf[:, cols],
            preferred_element_type=jnp.float32,
        )

    def pair_copy(u, dx):
        return pltpu.make_async_remote_copy(
            src_ref=pair_send.at[u, dx], dst_ref=pair_recv.at[u, dx],
            send_sem=pair_ssem.at[u, dx], recv_sem=pair_rsem.at[u, dx],
            device_id={"head": partner}, device_id_type=MESH,
        )

    def x_copy(u, dx):
        return pltpu.make_async_remote_copy(
            src_ref=x_send.at[u, dx - 1], dst_ref=x_recv.at[u, dx - 1],
            send_sem=x_ssem.at[u, dx - 1], recv_sem=x_rsem.at[u, dx - 1],
            device_id={"head": lax.rem(xi + dx, X) * 2 + core}, device_id_type=MESH,
        )

    def kv_at(u, block):
        j, th = units[u]
        return kv.at[block, j, pl.ds(th * nt, nt)]

    def z_copy(u, direction, step, block):
        to = lax.rem(t + 1, T) if direction == 0 else lax.rem(t + T - 1, T)
        return pltpu.make_async_remote_copy(
            src_ref=kv_at(u, block), dst_ref=kv_at(u, block),
            send_sem=z_ssem.at[direction, step, u], recv_sem=z_rsem.at[direction, step, u],
            device_id={"tok": to}, device_id_type=MESH,
        )

    def can_send(direction, step, j):
        end = 1 if j == moved else 0
        if direction == 0:
            return jnp.logical_and(t + 1 < T - end, t - step >= 0)
        return jnp.logical_and(t - 1 >= end, t + step < T)

    def can_recv(direction, step, j):
        end = 1 if j == moved else 0
        if direction == 0:
            return jnp.logical_and(t < T - end, t - 1 - step >= 0)
        return jnp.logical_and(t >= end, t + 1 + step < T)

    def arriving(direction, step):
        block = t - 1 - step if direction == 0 else t + 1 + step
        return jnp.clip(block, 0, T - 1)

    def leaving(direction, step):
        block = t - step if direction == 0 else t + step
        return jnp.clip(block, 0, T - 1)

    def stage_matmul(u):
        j, th = units[u]
        for dx in list(range(1, X)) + [0]:
            to = lax.rem(xi + dx, X)
            pair_send[u, dx] = project(j, th, to * 2 + (1 - core))
            pair_copy(u, dx).start()
            keep[u, dx] = project(j, th, to * 2 + core)

    def stage_chip(u):
        for dx in range(1, X):
            pair_copy(u, dx).wait_recv()
            x_send[u, dx - 1] = (keep[u, dx] + pair_recv[u, dx]).astype(WIRE)
            x_copy(u, dx).start()

    def stage_finish(u):
        j, th = units[u]
        pair_copy(u, 0).wait_recv()
        whole = keep[u, 0] + pair_recv[u, 0]
        for dx in range(1, X):
            x_copy(u, dx).wait_recv()
            whole = whole + x_recv[u, dx - 1].astype(jnp.float32)
        cosine = cos_buf[th * nt:(th + 1) * nt]
        sine = sin_buf[th * nt:(th + 1) * nt]
        k = whole[:, :HD]
        k = k * cosine + pltpu.roll(k, half, 1) * sine
        rows_at = slice(th * nt, (th + 1) * nt)
        kv[pl.ds(t, 1), j, rows_at, :HD] = k.astype(jnp.bfloat16)[None]
        kv[pl.ds(t, 1), j, rows_at, HD:] = whole[:, HD:].astype(jnp.bfloat16)[None]
        for direction in range(2):
            @pl.when(can_send(direction, 0, j))
            def _():
                z_copy(u, direction, 0, t).start()

    n_units = len(units)
    for u in range(n_units):
        j, th = units[u]
        if th == 0:
            for c in w_loads[order.index(j)]:
                c.wait()
        stage_matmul(u)
        stage_chip(u)
        if u > 0:
            stage_finish(u - 1)
    stage_finish(n_units - 1)

    for c in pos_copies:
        c.wait()
    if offload:
        @pl.when(is_helper)
        def _():
            for c in ask_copies():
                c.wait_recv()
            mask_extra[...] = jnp.broadcast_to(
                len_extra[...].astype(jnp.float32), (HD, rows)
            ).T.astype(jnp.int32)

    heads = kv_here * QPK
    top_lanes[...] = jnp.full(top_lanes.shape, -1e30, jnp.float32)
    numer[...] = jnp.zeros(numer.shape, jnp.float32)
    denom[...] = jnp.zeros(denom.shape, jnp.float32)
    scale = HD ** (-0.5)

    def score_block(block, j, extra=False):
        k = kv[block, j, :, :HD]
        valid = pos_all[block] < (mask_extra if extra else mask_len)[:, :1]
        for g in range(QPK):
            e = heads + g if extra else j * QPK + g
            if extra:
                q = q_extra[:, g * HD:(g + 1) * HD]
            else:
                q = qbuf[:, e * HD:(e + 1) * HD]
            s = lax.dot_general(
                q, k, (((1,), (1,)), ((), ())), preferred_element_type=jnp.float32
            ) * scale
            s = jnp.where(valid, s, -1e30)
            scores[block, e] = s
            top_lanes[e] = jnp.maximum(top_lanes[e], jnp.max(s, axis=1, keepdims=True))

    def value_block(block, j, extra=False):
        v = kv[block, j, :, HD:]
        for g in range(QPK):
            e = heads + g if extra else j * QPK + g
            w = jnp.exp(scores[block, e] - top_lanes[e][:, :1]).astype(jnp.bfloat16)
            denom[e] += jnp.sum(w.astype(jnp.float32), axis=1, keepdims=True)
            numer[e] += jnp.dot(w, v, preferred_element_type=jnp.float32)

    def arrive(j, direction, step):
        for u in range(n_units):
            if units[u][0] != j:
                continue
            z_copy(u, direction, step, arriving(direction, step)).wait_recv()
            if step + 1 < T - 1:
                @pl.when(can_send(direction, step + 1, j))
                def _():
                    z_copy(u, direction, step + 1, leaving(direction, step + 1)).start()

    def values_of(j):
        value_block(t, j)
        for step in range(T - 1):
            for direction in range(2):
                @pl.when(can_recv(direction, step, j))
                def _():
                    value_block(arriving(direction, step), j)

    def serves(direction):
        return t == T - 2 if direction == 0 else t == 1

    def answer():
        value_block(t, moved, extra=True)
        for direction in range(2):
            @pl.when(serves(direction))
            def _():
                for step in range(T - 2):
                    value_block(arriving(direction, step), moved, extra=True)
        for g in range(QPK):
            e = heads + g
            far_out[g] = (numer[e] / denom[e]).astype(jnp.bfloat16)
            far_stats[0, g:g + 1] = top_lanes[e].T[0:1]
            far_stats[1, g:g + 1] = denom[e].T[0:1]
        for c in answer_copies():
            c.start()

    for j in order:
        score_block(t, j)
    if offload:
        @pl.when(is_helper)
        def _():
            score_block(t, moved, extra=True)
    for step in range(T - 1):
        for j in order:
            for direction in range(2):
                @pl.when(can_recv(direction, step, j))
                def _():
                    arrive(j, direction, step)
                    score_block(arriving(direction, step), j)
                if j == moved and step < T - 2:
                    @pl.when(serves(direction))
                    def _():
                        score_block(arriving(direction, step), j, extra=True)
            if j == moved and step == T - 3:
                @pl.when(is_helper)
                def _():
                    answer()
            if step == T - 2 and j != order[-1]:
                values_of(j)
    values_of(order[-1])
    for e in range(heads):
        if e // QPK != moved:
            out_ref[:, e * HD:(e + 1) * HD] = (numer[e] / denom[e]).astype(jnp.bfloat16)
    if offload:
        @pl.when(is_client)
        def _():
            for c in answer_copies():
                c.wait_recv()
            for g in range(QPK):
                e = moved * QPK + g
                far_top = jnp.broadcast_to(near_stats[0, g:g + 1], (HD, rows)).T
                far_den = jnp.broadcast_to(near_stats[1, g:g + 1], (HD, rows)).T
                top = jnp.maximum(top_lanes[e], far_top)
                a = jnp.exp(top_lanes[e] - top)
                b = jnp.exp(far_top - top) * far_den
                numer[e] = numer[e] * a + near_out[g].astype(jnp.float32) * b
                denom[e] = denom[e] * a + b
        for g in range(QPK):
            e = moved * QPK + g
            out_ref[:, e * HD:(e + 1) * HD] = (numer[e] / denom[e]).astype(jnp.bfloat16)

        @pl.when(is_client)
        def _():
            for c in ask_copies():
                c.wait_send()

        @pl.when(is_helper)
        def _():
            for c in answer_copies():
                c.wait_send()

    for u in range(n_units):
        for dx in range(X):
            pair_copy(u, dx).wait_send()
        for dx in range(1, X):
            x_copy(u, dx).wait_send()
        for step in range(T - 1):
            for direction in range(2):
                @pl.when(can_send(direction, step, units[u][0]))
                def _():
                    z_copy(u, direction, step, leaving(direction, step)).wait_send()


def body(hidden, positions, norm_gain, w_key, w_value, queries, lengths):
    T, H = lax.axis_size("tok"), lax.axis_size("head")
    X = H // 2
    n_tok, width = hidden.shape
    rows, q_cols = queries.shape
    kw = 2 * HD
    kv_here = w_key.shape[1] // HD // H
    e = q_cols // HD
    ex = e + QPK
    nt = n_tok // TOK_SPLIT
    n_units = kv_here * TOK_SPLIT
    f32, bf16 = jnp.float32, jnp.bfloat16
    vmem = pl.BlockSpec(memory_space=pltpu.VMEM)
    hbm = pl.BlockSpec(memory_space=pl.ANY)
    dma = pltpu.SemaphoreType.DMA
    scratch = [
        pltpu.VMEM((n_tok, width), bf16),
        pltpu.VMEM((n_tok, width), bf16),
        pltpu.VMEM((width, 2 * w_key.shape[1]), bf16),
        pltpu.VMEM((rows, q_cols), bf16),
        pltpu.VMEM((H, 8, n_tok), f32),
        pltpu.VMEM((n_tok, HD), f32),
        pltpu.VMEM((n_tok, HD), f32),
        pltpu.VMEM((T, 1, n_tok), jnp.int32),
        pltpu.VMEM((rows, HD), jnp.int32),
        pltpu.VMEM((n_units, X, nt, kw), f32),
        pltpu.VMEM((n_units, X, nt, kw), f32),
        pltpu.VMEM((n_units, X, nt, kw), f32),
        pltpu.VMEM((n_units, X - 1, nt, kw), WIRE),
        pltpu.VMEM((n_units, X - 1, nt, kw), WIRE),
        pltpu.VMEM((T, kv_here, n_tok, kw), bf16),
        pltpu.VMEM((T, ex, rows, n_tok), f32),
        pltpu.VMEM((ex, rows, HD), f32),
        pltpu.VMEM((ex, rows, HD), f32),
        pltpu.VMEM((ex, rows, HD), f32),
        dma((1 + H_PARTS + 2 * H * kv_here,)),
        dma((H,)), dma((H,)),
        dma((T,)), dma((T,)),
        dma((n_units, X)), dma((n_units, X)),
        dma((n_units, X - 1)), dma((n_units, X - 1)),
        dma((2, T - 1, n_units)), dma((2, T - 1, n_units)),
        pltpu.VMEM((rows, QPK * HD), bf16),
        pltpu.VMEM((1, rows), jnp.int32),
        pltpu.VMEM((rows, HD), jnp.int32),
        pltpu.VMEM((QPK, rows, HD), bf16),
        pltpu.VMEM((2, QPK, rows), f32),
        pltpu.VMEM((QPK, rows, HD), bf16),
        pltpu.VMEM((2, QPK, rows), f32),
        dma((4,)), dma((4,)),
    ]
    return pl.pallas_call(
        functools.partial(kernel, T, H, width * H),
        out_shape=jax.ShapeDtypeStruct((rows, q_cols), bf16),
        in_specs=[hbm, vmem, vmem, hbm, hbm, hbm, vmem],
        out_specs=vmem,
        scratch_shapes=scratch,
        compiler_params=pltpu.CompilerParams(
            collective_id=0, has_side_effects=True, vmem_limit_bytes=60 * 1024 * 1024
        ),
    )(
        hidden, positions.reshape(1, n_tok), norm_gain.reshape(1, width), w_key, w_value,
        queries, lengths.reshape(1, rows),
    )


def solution(mesh):
    in_specs = (
        P(("groups", "tok"), "head"),
        P(("groups", "tok")),
        P("head"),
        P("head", None),
        P("head", None),
        P(("groups", "tok"), "head"),
        P(("groups", "tok")),
    )
    out_specs = P(("groups", "tok"), "head")
    return jax.shard_map(body, mesh=mesh, in_specs=in_specs, out_specs=out_specs, check_vma=False)
```

```python
import functools

import jax
import jax.numpy as jnp
from jax import lax
from jax.experimental import pallas as pl
from jax.experimental.pallas import tpu as pltpu
from jax.sharding import PartitionSpec as P

HD = 128
QPK = 8
THETA = 500000.0
EPS = 1e-05
H_PARTS = 4
TOK_SPLIT = 2
WIRE = jnp.bfloat16
MESH = pl.DeviceIdType.MESH


def kernel(
    T, H, full_width,
    hidden_hbm, pos_ref, gain_ref, wk_hbm, wv_hbm, q_hbm, len_ref,
    out_ref,
    hid, normed, wbuf, qbuf, squares, cos_buf, sin_buf, pos_all, mask_len,
    pair_send, pair_recv, keep, x_send, x_recv, kv, scores, top_lanes, numer, denom,
    load_sem, sq_send, sq_recv, pos_send, pos_recv,
    pair_ssem, pair_rsem, x_ssem, x_rsem, z_ssem, z_rsem,
    q_extra, len_extra, mask_extra, far_out, far_stats, near_out, near_stats, off_ssem, off_rsem,
    q_stack,
):
    X = H // 2
    n_tok, width = hid.shape
    kw = kv.shape[-1]
    kv_here = kv.shape[1]
    rows = qbuf.shape[0]
    nt = n_tok // TOK_SPLIT
    t = lax.axis_index("tok")
    head = lax.axis_index("head")
    xi, core = head // 2, lax.rem(head, 2)
    partner = xi * 2 + (1 - core)
    order = list(reversed(range(kv_here)))
    offload = kv_here > 1 and T >= 4
    moved = kv_here - 1 if offload else -1
    is_client = jnp.logical_or(t == 0, t == T - 1)
    is_helper = jnp.logical_or(t == 1, t == T - 2)
    other_end = jnp.where(t < T // 2, jnp.where(t == 0, 1, 0), jnp.where(t == T - 1, T - 2, T - 1))

    part = n_tok // H_PARTS
    h_loads = [
        pltpu.make_async_copy(
            hidden_hbm.at[pl.ds(i * part, part)], hid.at[pl.ds(i * part, part)], load_sem.at[1 + i]
        )
        for i in range(H_PARTS)
    ]
    w_loads = []
    at = 1 + H_PARTS
    for j in order:
        group = []
        for blk in range(H):
            for which, src in enumerate((wk_hbm, wv_hbm)):
                h = blk * kv_here + j
                group.append(
                    pltpu.make_async_copy(
                        src.at[:, pl.ds(h * HD, HD)],
                        wbuf.at[:, pl.ds(h * kw + which * HD, HD)],
                        load_sem.at[at],
                    )
                )
                at += 1
        w_loads.append(group)
    q_load = pltpu.make_async_copy(q_hbm, qbuf, load_sem.at[0])
    for c in h_loads:
        c.start()
    q_load.start()

    barrier = pltpu.get_barrier_semaphore()
    for d in range(1, H):
        pl.semaphore_signal(
            barrier, inc=1, device_id={"head": lax.rem(head + d, H)}, device_id_type=MESH
        )
    for d in range(1, T):
        pl.semaphore_signal(
            barrier, inc=1, device_id={"tok": lax.rem(t + d, T)}, device_id_type=MESH
        )

    pos_row = pos_ref[...].reshape(1, n_tok)
    pos_all[pl.ds(t, 1)] = pos_row[None]

    sums = []
    for p in range(H_PARTS):
        h_loads[p].wait()
        acc = jnp.zeros((part, HD), jnp.float32)
        for i in range(width // HD):
            piece = hid[p * part:(p + 1) * part, i * HD:(i + 1) * HD].astype(jnp.float32)
            acc = acc + piece * piece
        sums.append(acc)
    for group in w_loads:
        for c in group:
            c.start()
    acc = jnp.concatenate(sums, axis=0)
    local = jnp.sum(acc.T, axis=0, keepdims=True)
    squares[pl.ds(head, 1)] = local[None]

    pl.semaphore_wait(barrier, H - 1 + T - 1)
    sq_copies = []
    for d in range(1, H):
        c = pltpu.make_async_remote_copy(
            src_ref=squares.at[head], dst_ref=squares.at[head],
            send_sem=sq_send.at[d], recv_sem=sq_recv.at[d],
            device_id={"head": lax.rem(head + d, H)}, device_id_type=MESH,
        )
        c.start()
        sq_copies.append(c)
    pos_copies = []
    for d in range(1, T):
        c = pltpu.make_async_remote_copy(
            src_ref=pos_all.at[t], dst_ref=pos_all.at[t],
            send_sem=pos_send.at[d], recv_sem=pos_recv.at[d],
            device_id={"tok": lax.rem(t + d, T)}, device_id_type=MESH,
        )
        c.start()
        pos_copies.append(c)

    def off_copy(i, src, dst):
        return pltpu.make_async_remote_copy(
            src_ref=src, dst_ref=dst, send_sem=off_ssem.at[i], recv_sem=off_rsem.at[i],
            device_id={"tok": other_end}, device_id_type=MESH,
        )

    def ask_copies():
        cols = pl.ds(moved * QPK * HD, QPK * HD)
        return off_copy(0, qbuf.at[:, cols], q_extra), off_copy(1, len_ref, len_extra)

    def answer_copies():
        return off_copy(2, far_out, near_out), off_copy(3, far_stats, near_stats)

    q_load.wait()
    if offload:
        @pl.when(is_client)
        def _():
            for c in ask_copies():
                c.start()

    pos_col = jnp.broadcast_to(pos_row.astype(jnp.float32), (HD, n_tok)).T
    lane = lax.broadcasted_iota(jnp.int32, (1, HD), 1)
    half = HD // 2
    idx = jnp.where(lane < half, lane, lane - half).astype(jnp.float32)
    freq = THETA ** (-(idx * 2.0) / HD)
    angle = pos_col * freq
    cos_buf[...] = jnp.cos(angle)
    sine = jnp.sin(angle)
    sin_buf[...] = jnp.where(lane < half, -sine, sine)
    mask_len[...] = jnp.broadcast_to(len_ref[...].astype(jnp.float32), (HD, rows)).T.astype(jnp.int32)

    for e in range(kv_here * QPK):
        q_stack[e] = qbuf[:, e * HD:(e + 1) * HD]

    for c in sq_copies:
        c.wait()
    total = squares[0]
    for i in range(1, H):
        total = total + squares[i]
    r = lax.rsqrt(total / full_width + EPS)
    r_col = jnp.broadcast_to(r, (HD, n_tok)).T
    for i in range(width // HD):
        cols = slice(i * HD, (i + 1) * HD)
        wide = hid[:, cols].astype(jnp.float32)
        normed[:, cols] = (wide * r_col * gain_ref[:, cols]).astype(jnp.bfloat16)

    units = [(j, th) for j in order for th in range(TOK_SPLIT)]

    def project(j, th, block):
        cols = pl.ds(pl.multiple_of((block * kv_here + j) * kw, kw), kw)
        return jnp.dot(
            normed[th * nt:(th + 1) * nt, :], wbuf[:, cols],
            preferred_element_type=jnp.float32,
        )

    def pair_copy(u, dx):
        return pltpu.make_async_remote_copy(
            src_ref=pair_send.at[u, dx], dst_ref=pair_recv.at[u, dx],
            send_sem=pair_ssem.at[u, dx], recv_sem=pair_rsem.at[u, dx],
            device_id={"head": partner}, device_id_type=MESH,
        )

    def x_copy(u, dx):
        return pltpu.make_async_remote_copy(
            src_ref=x_send.at[u, dx - 1], dst_ref=x_recv.at[u, dx - 1],
            send_sem=x_ssem.at[u, dx - 1], recv_sem=x_rsem.at[u, dx - 1],
            device_id={"head": lax.rem(xi + dx, X) * 2 + core}, device_id_type=MESH,
        )

    def kv_at(u, block):
        j, th = units[u]
        return kv.at[block, j, pl.ds(th * nt, nt)]

    def z_copy(u, direction, step, block):
        to = lax.rem(t + 1, T) if direction == 0 else lax.rem(t + T - 1, T)
        return pltpu.make_async_remote_copy(
            src_ref=kv_at(u, block), dst_ref=kv_at(u, block),
            send_sem=z_ssem.at[direction, step, u], recv_sem=z_rsem.at[direction, step, u],
            device_id={"tok": to}, device_id_type=MESH,
        )

    def can_send(direction, step, j):
        end = 1 if j == moved else 0
        if direction == 0:
            return jnp.logical_and(t + 1 < T - end, t - step >= 0)
        return jnp.logical_and(t - 1 >= end, t + step < T)

    def can_recv(direction, step, j):
        end = 1 if j == moved else 0
        if direction == 0:
            return jnp.logical_and(t < T - end, t - 1 - step >= 0)
        return jnp.logical_and(t >= end, t + 1 + step < T)

    def arriving(direction, step):
        block = t - 1 - step if direction == 0 else t + 1 + step
        return jnp.clip(block, 0, T - 1)

    def leaving(direction, step):
        block = t - step if direction == 0 else t + step
        return jnp.clip(block, 0, T - 1)

    def stage_matmul(u):
        j, th = units[u]
        for dx in list(range(1, X)) + [0]:
            to = lax.rem(xi + dx, X)
            pair_send[u, dx] = project(j, th, to * 2 + (1 - core))
            pair_copy(u, dx).start()
            keep[u, dx] = project(j, th, to * 2 + core)

    def stage_chip(u):
        for dx in range(1, X):
            pair_copy(u, dx).wait_recv()
            x_send[u, dx - 1] = (keep[u, dx] + pair_recv[u, dx]).astype(WIRE)
            x_copy(u, dx).start()

    def stage_finish(u):
        j, th = units[u]
        pair_copy(u, 0).wait_recv()
        whole = keep[u, 0] + pair_recv[u, 0]
        for dx in range(1, X):
            x_copy(u, dx).wait_recv()
            whole = whole + x_recv[u, dx - 1].astype(jnp.float32)
        cosine = cos_buf[th * nt:(th + 1) * nt]
        sine = sin_buf[th * nt:(th + 1) * nt]
        k = whole[:, :HD]
        k = k * cosine + pltpu.roll(k, half, 1) * sine
        rows_at = slice(th * nt, (th + 1) * nt)
        kv[pl.ds(t, 1), j, rows_at, :HD] = k.astype(jnp.bfloat16)[None]
        kv[pl.ds(t, 1), j, rows_at, HD:] = whole[:, HD:].astype(jnp.bfloat16)[None]
        for direction in range(2):
            @pl.when(can_send(direction, 0, j))
            def _():
                z_copy(u, direction, 0, t).start()

    n_units = len(units)
    for u in range(n_units):
        j, th = units[u]
        if th == 0:
            for c in w_loads[order.index(j)]:
                c.wait()
        stage_matmul(u)
        stage_chip(u)
    for u in range(n_units):
        stage_finish(u)

    for c in pos_copies:
        c.wait()
    if offload:
        @pl.when(is_helper)
        def _():
            for c in ask_copies():
                c.wait_recv()
            mask_extra[...] = jnp.broadcast_to(
                len_extra[...].astype(jnp.float32), (HD, rows)
            ).T.astype(jnp.int32)
            for g in range(QPK):
                q_stack[kv_here * QPK + g] = q_extra[:, g * HD:(g + 1) * HD]

    heads = kv_here * QPK
    top_lanes[...] = jnp.full(top_lanes.shape, -1e30, jnp.float32)
    numer[...] = jnp.zeros(numer.shape, jnp.float32)
    denom[...] = jnp.zeros(denom.shape, jnp.float32)
    scale = HD ** (-0.5)

    group = QPK // 2

    def score_block(block, j, extra=False):
        k = kv[block, j, :, :HD]
        valid = (pos_all[block] < (mask_extra if extra else mask_len)[:, :1])[None]
        slot = kv_here if extra else j
        for half_at in range(0, QPK, group):
            e = slice(slot * QPK + half_at, slot * QPK + half_at + group)
            q = q_stack[e].reshape(group * rows, HD)
            s = lax.dot_general(
                q, k, (((1,), (1,)), ((), ())), preferred_element_type=jnp.float32
            ).reshape(group, rows, n_tok) * scale
            s = jnp.where(valid, s, -1e30)
            scores[block, e] = s
            top_lanes[e] = jnp.maximum(top_lanes[e], jnp.max(s, axis=2, keepdims=True))

    def value_block(block, j, extra=False):
        v = kv[block, j, :, HD:]
        v = jnp.concatenate([v, jnp.ones(v.shape, v.dtype)], axis=1)
        slot = kv_here if extra else j
        for half_at in range(0, QPK, group):
            e = slice(slot * QPK + half_at, slot * QPK + half_at + group)
            w = jnp.exp(scores[block, e] - top_lanes[e][:, :, :1]).astype(jnp.bfloat16)
            both = jnp.dot(
                w.reshape(group * rows, n_tok), v, preferred_element_type=jnp.float32
            ).reshape(group, rows, 2 * HD)
            numer[e] += both[:, :, :HD]
            denom[e] += both[:, :, HD:]

    def arrive(j, direction, step):
        for u in range(n_units):
            if units[u][0] != j:
                continue
            z_copy(u, direction, step, arriving(direction, step)).wait_recv()
            if step + 1 < T - 1:
                @pl.when(can_send(direction, step + 1, j))
                def _():
                    z_copy(u, direction, step + 1, leaving(direction, step + 1)).start()

    def values_of(j):
        value_block(t, j)
        for step in range(T - 1):
            for direction in range(2):
                @pl.when(can_recv(direction, step, j))
                def _():
                    value_block(arriving(direction, step), j)

    def serves(direction):
        return t == T - 2 if direction == 0 else t == 1

    def answer():
        value_block(t, moved, extra=True)
        for direction in range(2):
            @pl.when(serves(direction))
            def _():
                for step in range(T - 2):
                    value_block(arriving(direction, step), moved, extra=True)
        for g in range(QPK):
            e = heads + g
            far_out[g] = (numer[e] / denom[e]).astype(jnp.bfloat16)
            far_stats[0, g:g + 1] = top_lanes[e].T[0:1]
            far_stats[1, g:g + 1] = denom[e].T[0:1]
        for c in answer_copies():
            c.start()

    for j in order:
        score_block(t, j)
    if offload:
        @pl.when(is_helper)
        def _():
            score_block(t, moved, extra=True)
    for step in range(T - 1):
        for j in order:
            for direction in range(2):
                @pl.when(can_recv(direction, step, j))
                def _():
                    arrive(j, direction, step)
                    score_block(arriving(direction, step), j)
                if j == moved and step < T - 2:
                    @pl.when(serves(direction))
                    def _():
                        score_block(arriving(direction, step), j, extra=True)
            if j == moved and step == T - 3:
                @pl.when(is_helper)
                def _():
                    answer()
            if step == T - 2 and j != order[-1]:
                values_of(j)
    values_of(order[-1])
    for e in range(heads):
        if e // QPK != moved:
            out_ref[:, e * HD:(e + 1) * HD] = (numer[e] / denom[e]).astype(jnp.bfloat16)
    if offload:
        @pl.when(is_client)
        def _():
            for c in answer_copies():
                c.wait_recv()
            for g in range(QPK):
                e = moved * QPK + g
                far_top = jnp.broadcast_to(near_stats[0, g:g + 1], (HD, rows)).T
                far_den = jnp.broadcast_to(near_stats[1, g:g + 1], (HD, rows)).T
                top = jnp.maximum(top_lanes[e], far_top)
                a = jnp.exp(top_lanes[e] - top)
                b = jnp.exp(far_top - top) * far_den
                numer[e] = numer[e] * a + near_out[g].astype(jnp.float32) * b
                denom[e] = denom[e] * a + b
        for g in range(QPK):
            e = moved * QPK + g
            out_ref[:, e * HD:(e + 1) * HD] = (numer[e] / denom[e]).astype(jnp.bfloat16)

        @pl.when(is_client)
        def _():
            for c in ask_copies():
                c.wait_send()

        @pl.when(is_helper)
        def _():
            for c in answer_copies():
                c.wait_send()

    for u in range(n_units):
        for dx in range(X):
            pair_copy(u, dx).wait_send()
        for dx in range(1, X):
            x_copy(u, dx).wait_send()
        for step in range(T - 1):
            for direction in range(2):
                @pl.when(can_send(direction, step, units[u][0]))
                def _():
                    z_copy(u, direction, step, leaving(direction, step)).wait_send()


def body(hidden, positions, norm_gain, w_key, w_value, queries, lengths):
    T, H = lax.axis_size("tok"), lax.axis_size("head")
    X = H // 2
    n_tok, width = hidden.shape
    rows, q_cols = queries.shape
    kw = 2 * HD
    kv_here = w_key.shape[1] // HD // H
    e = q_cols // HD
    ex = e + QPK
    nt = n_tok // TOK_SPLIT
    n_units = kv_here * TOK_SPLIT
    f32, bf16 = jnp.float32, jnp.bfloat16
    vmem = pl.BlockSpec(memory_space=pltpu.VMEM)
    hbm = pl.BlockSpec(memory_space=pl.ANY)
    dma = pltpu.SemaphoreType.DMA
    scratch = [
        pltpu.VMEM((n_tok, width), bf16),
        pltpu.VMEM((n_tok, width), bf16),
        pltpu.VMEM((width, 2 * w_key.shape[1]), bf16),
        pltpu.VMEM((rows, q_cols), bf16),
        pltpu.VMEM((H, 1, n_tok), f32),
        pltpu.VMEM((n_tok, HD), f32),
        pltpu.VMEM((n_tok, HD), f32),
        pltpu.VMEM((T, 1, n_tok), jnp.int32),
        pltpu.VMEM((rows, HD), jnp.int32),
        pltpu.VMEM((n_units, X, nt, kw), f32),
        pltpu.VMEM((n_units, X, nt, kw), f32),
        pltpu.VMEM((n_units, X, nt, kw), f32),
        pltpu.VMEM((n_units, X - 1, nt, kw), WIRE),
        pltpu.VMEM((n_units, X - 1, nt, kw), WIRE),
        pltpu.VMEM((T, kv_here, n_tok, kw), bf16),
        pltpu.VMEM((T, ex, rows, n_tok), f32),
        pltpu.VMEM((ex, rows, HD), f32),
        pltpu.VMEM((ex, rows, HD), f32),
        pltpu.VMEM((ex, rows, HD), f32),
        dma((1 + H_PARTS + 2 * H * kv_here,)),
        dma((H,)), dma((H,)),
        dma((T,)), dma((T,)),
        dma((n_units, X)), dma((n_units, X)),
        dma((n_units, X - 1)), dma((n_units, X - 1)),
        dma((2, T - 1, n_units)), dma((2, T - 1, n_units)),
        pltpu.VMEM((rows, QPK * HD), bf16),
        pltpu.VMEM((1, rows), jnp.int32),
        pltpu.VMEM((rows, HD), jnp.int32),
        pltpu.VMEM((QPK, rows, HD), bf16),
        pltpu.VMEM((2, QPK, rows), f32),
        pltpu.VMEM((QPK, rows, HD), bf16),
        pltpu.VMEM((2, QPK, rows), f32),
        dma((4,)), dma((4,)),
        pltpu.VMEM((ex, rows, HD), bf16),
    ]
    return pl.pallas_call(
        functools.partial(kernel, T, H, width * H),
        out_shape=jax.ShapeDtypeStruct((rows, q_cols), bf16),
        in_specs=[hbm, vmem, vmem, hbm, hbm, hbm, vmem],
        out_specs=vmem,
        scratch_shapes=scratch,
        compiler_params=pltpu.CompilerParams(
            collective_id=0, has_side_effects=True, vmem_limit_bytes=60 * 1024 * 1024
        ),
    )(
        hidden, positions, norm_gain.reshape(1, width), w_key, w_value,
        queries, lengths.reshape(1, rows),
    )


def solution(mesh):
    in_specs = (
        P(("groups", "tok"), "head"),
        P(("groups", "tok")),
        P("head"),
        P("head", None),
        P("head", None),
        P(("groups", "tok"), "head"),
        P(("groups", "tok")),
    )
    out_specs = P(("groups", "tok"), "head")
    return jax.shard_map(body, mesh=mesh, in_specs=in_specs, out_specs=out_specs, check_vma=False)
```

```python
import functools

import jax
import jax.numpy as jnp
from jax import lax
from jax.experimental import pallas as pl
from jax.experimental.pallas import tpu as pltpu
from jax.sharding import PartitionSpec as P

HD = 128
QPK = 8
THETA = 500000.0
EPS = 1e-05
H_PARTS = 4
TOK_SPLIT = 2
WIRE = jnp.bfloat16
MESH = pl.DeviceIdType.MESH


def kernel(
    T, H, full_width,
    hidden_hbm, pos_ref, gain_ref, wk_hbm, wv_hbm, q_hbm, len_ref,
    out_ref,
    hid, normed, wbuf, qbuf, squares, cos_buf, sin_buf, pos_all, mask_len,
    pair_send, pair_recv, keep, x_send, x_recv, kv, scores, top_lanes, numer, denom,
    load_sem, sq_send, sq_recv, pos_send, pos_recv,
    pair_ssem, pair_rsem, x_ssem, x_rsem, z_ssem, z_rsem,
    q_extra, len_extra, mask_extra, far_out, far_stats, near_out, near_stats, off_ssem, off_rsem,
    q_stack,
):
    X = H // 2
    n_tok, width = hid.shape
    kw = kv.shape[-1]
    kv_here = kv.shape[1]
    rows = qbuf.shape[0]
    nt = n_tok // TOK_SPLIT
    t = lax.axis_index("tok")
    head = lax.axis_index("head")
    xi, core = head // 2, lax.rem(head, 2)
    partner = xi * 2 + (1 - core)
    order = list(reversed(range(kv_here)))
    offload = kv_here > 1 and T >= 4
    moved = kv_here - 1 if offload else -1
    is_client = jnp.logical_or(t == 0, t == T - 1)
    is_helper = jnp.logical_or(t == 1, t == T - 2)
    other_end = jnp.where(t < T // 2, jnp.where(t == 0, 1, 0), jnp.where(t == T - 1, T - 2, T - 1))

    part = n_tok // H_PARTS
    h_loads = [
        pltpu.make_async_copy(
            hidden_hbm.at[pl.ds(i * part, part)], hid.at[pl.ds(i * part, part)], load_sem.at[1 + i]
        )
        for i in range(H_PARTS)
    ]
    w_loads = []
    at = 1 + H_PARTS
    for j in order:
        group = []
        for blk in range(H):
            for which, src in enumerate((wk_hbm, wv_hbm)):
                h = blk * kv_here + j
                group.append(
                    pltpu.make_async_copy(
                        src.at[:, pl.ds(h * HD, HD)],
                        wbuf.at[:, pl.ds(h * kw + which * HD, HD)],
                        load_sem.at[at],
                    )
                )
                at += 1
        w_loads.append(group)
    q_load = pltpu.make_async_copy(q_hbm, qbuf, load_sem.at[0])
    for c in h_loads:
        c.start()
    q_load.start()

    barrier = pltpu.get_barrier_semaphore()
    for d in range(1, H):
        pl.semaphore_signal(
            barrier, inc=1, device_id={"head": lax.rem(head + d, H)}, device_id_type=MESH
        )
    for d in range(1, T):
        pl.semaphore_signal(
            barrier, inc=1, device_id={"tok": lax.rem(t + d, T)}, device_id_type=MESH
        )

    pos_row = pos_ref[...].reshape(1, n_tok)
    pos_all[pl.ds(t, 1)] = pos_row[None]

    sums = []
    for p in range(H_PARTS):
        h_loads[p].wait()
        acc = jnp.zeros((part, HD), jnp.float32)
        for i in range(width // HD):
            piece = hid[p * part:(p + 1) * part, i * HD:(i + 1) * HD].astype(jnp.float32)
            acc = acc + piece * piece
        sums.append(acc)
    for group in w_loads:
        for c in group:
            c.start()
    acc = jnp.concatenate(sums, axis=0)
    local = jnp.sum(acc.T, axis=0, keepdims=True)
    squares[pl.ds(head, 1)] = local[None]

    pl.semaphore_wait(barrier, H - 1 + T - 1)
    sq_copies = []
    for d in range(1, H):
        c = pltpu.make_async_remote_copy(
            src_ref=squares.at[head], dst_ref=squares.at[head],
            send_sem=sq_send.at[d], recv_sem=sq_recv.at[d],
            device_id={"head": lax.rem(head + d, H)}, device_id_type=MESH,
        )
        c.start()
        sq_copies.append(c)
    pos_copies = []
    for d in range(1, T):
        c = pltpu.make_async_remote_copy(
            src_ref=pos_all.at[t], dst_ref=pos_all.at[t],
            send_sem=pos_send.at[d], recv_sem=pos_recv.at[d],
            device_id={"tok": lax.rem(t + d, T)}, device_id_type=MESH,
        )
        c.start()
        pos_copies.append(c)

    def off_copy(i, src, dst):
        return pltpu.make_async_remote_copy(
            src_ref=src, dst_ref=dst, send_sem=off_ssem.at[i], recv_sem=off_rsem.at[i],
            device_id={"tok": other_end}, device_id_type=MESH,
        )

    def ask_copies():
        cols = pl.ds(moved * QPK * HD, QPK * HD)
        return off_copy(0, qbuf.at[:, cols], q_extra), off_copy(1, len_ref, len_extra)

    def answer_copies():
        return off_copy(2, far_out, near_out), off_copy(3, far_stats, near_stats)

    q_load.wait()
    if offload:
        @pl.when(is_client)
        def _():
            for c in ask_copies():
                c.start()

    pos_col = jnp.broadcast_to(pos_row.astype(jnp.float32), (HD, n_tok)).T
    lane = lax.broadcasted_iota(jnp.int32, (1, HD), 1)
    half = HD // 2
    idx = jnp.where(lane < half, lane, lane - half).astype(jnp.float32)
    freq = THETA ** (-(idx * 2.0) / HD)
    angle = pos_col * freq
    cos_buf[...] = jnp.cos(angle)
    sine = jnp.sin(angle)
    sin_buf[...] = jnp.where(lane < half, -sine, sine)
    mask_len[...] = jnp.broadcast_to(len_ref[...].astype(jnp.float32), (HD, rows)).T.astype(jnp.int32)

    for e in range(kv_here * QPK):
        q_stack[e] = qbuf[:, e * HD:(e + 1) * HD]

    for c in sq_copies:
        c.wait()
    total = squares[0]
    for i in range(1, H):
        total = total + squares[i]
    r = lax.rsqrt(total / full_width + EPS)
    r_col = jnp.broadcast_to(r, (HD, n_tok)).T
    for i in range(width // HD):
        cols = slice(i * HD, (i + 1) * HD)
        wide = hid[:, cols].astype(jnp.float32)
        normed[:, cols] = (wide * r_col * gain_ref[:, cols]).astype(jnp.bfloat16)

    units = [(j, th) for j in order for th in range(TOK_SPLIT)]

    def project(j, block):
        cols = pl.ds(pl.multiple_of((block * kv_here + j) * kw, kw), kw)
        return jnp.dot(
            normed[...], wbuf[:, cols],
            preferred_element_type=jnp.float32,
        )

    def pair_copy(u, dx):
        return pltpu.make_async_remote_copy(
            src_ref=pair_send.at[u, dx], dst_ref=pair_recv.at[u, dx],
            send_sem=pair_ssem.at[u, dx], recv_sem=pair_rsem.at[u, dx],
            device_id={"head": partner}, device_id_type=MESH,
        )

    def x_copy(u, dx):
        return pltpu.make_async_remote_copy(
            src_ref=x_send.at[u, dx - 1], dst_ref=x_recv.at[u, dx - 1],
            send_sem=x_ssem.at[u, dx - 1], recv_sem=x_rsem.at[u, dx - 1],
            device_id={"head": lax.rem(xi + dx, X) * 2 + core}, device_id_type=MESH,
        )

    def kv_at(u, block):
        j, th = units[u]
        return kv.at[block, j, pl.ds(th * nt, nt)]

    def z_copy(u, direction, step, block):
        to = lax.rem(t + 1, T) if direction == 0 else lax.rem(t + T - 1, T)
        return pltpu.make_async_remote_copy(
            src_ref=kv_at(u, block), dst_ref=kv_at(u, block),
            send_sem=z_ssem.at[direction, step, u], recv_sem=z_rsem.at[direction, step, u],
            device_id={"tok": to}, device_id_type=MESH,
        )

    def can_send(direction, step, j):
        end = 1 if j == moved else 0
        if direction == 0:
            return jnp.logical_and(t + 1 < T - end, t - step >= 0)
        return jnp.logical_and(t - 1 >= end, t + step < T)

    def can_recv(direction, step, j):
        end = 1 if j == moved else 0
        if direction == 0:
            return jnp.logical_and(t < T - end, t - 1 - step >= 0)
        return jnp.logical_and(t >= end, t + 1 + step < T)

    def arriving(direction, step):
        block = t - 1 - step if direction == 0 else t + 1 + step
        return jnp.clip(block, 0, T - 1)

    def leaving(direction, step):
        block = t - step if direction == 0 else t + step
        return jnp.clip(block, 0, T - 1)

    def stage_matmul(j):
        mine = [(u, units[u][1]) for u in range(len(units)) if units[u][0] == j]
        for dx in list(range(1, X)) + [0]:
            to = lax.rem(xi + dx, X)
            theirs = project(j, to * 2 + (1 - core))
            for u, th in mine:
                pair_send[u, dx] = theirs[th * nt:(th + 1) * nt]
                pair_copy(u, dx).start()
            ours = project(j, to * 2 + core)
            for u, th in mine:
                keep[u, dx] = ours[th * nt:(th + 1) * nt]

    def stage_chip(u):
        for dx in range(1, X):
            pair_copy(u, dx).wait_recv()
            x_send[u, dx - 1] = (keep[u, dx] + pair_recv[u, dx]).astype(WIRE)
            x_copy(u, dx).start()

    def stage_finish(u):
        j, th = units[u]
        pair_copy(u, 0).wait_recv()
        whole = keep[u, 0] + pair_recv[u, 0]
        for dx in range(1, X):
            x_copy(u, dx).wait_recv()
            whole = whole + x_recv[u, dx - 1].astype(jnp.float32)
        cosine = cos_buf[th * nt:(th + 1) * nt]
        sine = sin_buf[th * nt:(th + 1) * nt]
        k = whole[:, :HD]
        k = k * cosine + pltpu.roll(k, half, 1) * sine
        rows_at = slice(th * nt, (th + 1) * nt)
        kv[pl.ds(t, 1), j, rows_at, :HD] = k.astype(jnp.bfloat16)[None]
        kv[pl.ds(t, 1), j, rows_at, HD:] = whole[:, HD:].astype(jnp.bfloat16)[None]
        for direction in range(2):
            @pl.when(can_send(direction, 0, j))
            def _():
                z_copy(u, direction, 0, t).start()

    n_units = len(units)
    for at, j in enumerate(order):
        for c in w_loads[at]:
            c.wait()
        stage_matmul(j)
        for u in range(n_units):
            if units[u][0] == j:
                stage_chip(u)
    for u in range(n_units):
        stage_finish(u)

    for c in pos_copies:
        c.wait()
    if offload:
        @pl.when(is_helper)
        def _():
            for c in ask_copies():
                c.wait_recv()
            mask_extra[...] = jnp.broadcast_to(
                len_extra[...].astype(jnp.float32), (HD, rows)
            ).T.astype(jnp.int32)
            for g in range(QPK):
                q_stack[kv_here * QPK + g] = q_extra[:, g * HD:(g + 1) * HD]

    heads = kv_here * QPK
    top_lanes[...] = jnp.full(top_lanes.shape, -1e30, jnp.float32)
    numer[...] = jnp.zeros(numer.shape, jnp.float32)
    denom[...] = jnp.zeros(denom.shape, jnp.float32)
    scale = HD ** (-0.5)

    group = QPK // 2

    def score_block(block, j, extra=False):
        k = kv[block, j, :, :HD]
        valid = (pos_all[block] < (mask_extra if extra else mask_len)[:, :1])[None]
        slot = kv_here if extra else j
        for half_at in range(0, QPK, group):
            e = slice(slot * QPK + half_at, slot * QPK + half_at + group)
            q = q_stack[e].reshape(group * rows, HD)
            s = lax.dot_general(
                q, k, (((1,), (1,)), ((), ())), preferred_element_type=jnp.float32
            ).reshape(group, rows, n_tok) * scale
            s = jnp.where(valid, s, -1e30)
            scores[block, e] = s
            top_lanes[e] = jnp.maximum(top_lanes[e], jnp.max(s, axis=2, keepdims=True))

    def value_block(block, j, extra=False):
        v = kv[block, j, :, HD:]
        v = jnp.concatenate([v, jnp.ones(v.shape, v.dtype)], axis=1)
        slot = kv_here if extra else j
        for half_at in range(0, QPK, group):
            e = slice(slot * QPK + half_at, slot * QPK + half_at + group)
            w = jnp.exp(scores[block, e] - top_lanes[e][:, :, :1]).astype(jnp.bfloat16)
            both = jnp.dot(
                w.reshape(group * rows, n_tok), v, preferred_element_type=jnp.float32
            ).reshape(group, rows, 2 * HD)
            numer[e] += both[:, :, :HD]
            denom[e] += both[:, :, HD:]

    def arrive(j, direction, step):
        for u in range(n_units):
            if units[u][0] != j:
                continue
            z_copy(u, direction, step, arriving(direction, step)).wait_recv()
            if step + 1 < T - 1:
                @pl.when(can_send(direction, step + 1, j))
                def _():
                    z_copy(u, direction, step + 1, leaving(direction, step + 1)).start()

    def values_of(j):
        value_block(t, j)
        for step in range(T - 1):
            for direction in range(2):
                @pl.when(can_recv(direction, step, j))
                def _():
                    value_block(arriving(direction, step), j)

    def serves(direction):
        return t == T - 2 if direction == 0 else t == 1

    def answer():
        value_block(t, moved, extra=True)
        for direction in range(2):
            @pl.when(serves(direction))
            def _():
                for step in range(T - 2):
                    value_block(arriving(direction, step), moved, extra=True)
        for g in range(QPK):
            e = heads + g
            far_out[g] = (numer[e] / denom[e]).astype(jnp.bfloat16)
            far_stats[0, g:g + 1] = top_lanes[e].T[0:1]
            far_stats[1, g:g + 1] = denom[e].T[0:1]
        for c in answer_copies():
            c.start()

    for j in order:
        score_block(t, j)
    if offload:
        @pl.when(is_helper)
        def _():
            score_block(t, moved, extra=True)
    for step in range(T - 1):
        for j in order:
            for direction in range(2):
                @pl.when(can_recv(direction, step, j))
                def _():
                    arrive(j, direction, step)
                    score_block(arriving(direction, step), j)
                if j == moved and step < T - 2:
                    @pl.when(serves(direction))
                    def _():
                        score_block(arriving(direction, step), j, extra=True)
            if j == moved and step == T - 3:
                @pl.when(is_helper)
                def _():
                    answer()
            if step == T - 2 and j != order[-1]:
                values_of(j)
    values_of(order[-1])
    for e in range(heads):
        if e // QPK != moved:
            out_ref[:, e * HD:(e + 1) * HD] = (numer[e] / denom[e]).astype(jnp.bfloat16)
    if offload:
        @pl.when(is_client)
        def _():
            for c in answer_copies():
                c.wait_recv()
            for g in range(QPK):
                e = moved * QPK + g
                far_top = jnp.broadcast_to(near_stats[0, g:g + 1], (HD, rows)).T
                far_den = jnp.broadcast_to(near_stats[1, g:g + 1], (HD, rows)).T
                top = jnp.maximum(top_lanes[e], far_top)
                a = jnp.exp(top_lanes[e] - top)
                b = jnp.exp(far_top - top) * far_den
                numer[e] = numer[e] * a + near_out[g].astype(jnp.float32) * b
                denom[e] = denom[e] * a + b
        for g in range(QPK):
            e = moved * QPK + g
            out_ref[:, e * HD:(e + 1) * HD] = (numer[e] / denom[e]).astype(jnp.bfloat16)

        @pl.when(is_client)
        def _():
            for c in ask_copies():
                c.wait_send()

        @pl.when(is_helper)
        def _():
            for c in answer_copies():
                c.wait_send()

    for u in range(n_units):
        for dx in range(X):
            pair_copy(u, dx).wait_send()
        for dx in range(1, X):
            x_copy(u, dx).wait_send()
        for step in range(T - 1):
            for direction in range(2):
                @pl.when(can_send(direction, step, units[u][0]))
                def _():
                    z_copy(u, direction, step, leaving(direction, step)).wait_send()


def body(hidden, positions, norm_gain, w_key, w_value, queries, lengths):
    T, H = lax.axis_size("tok"), lax.axis_size("head")
    X = H // 2
    n_tok, width = hidden.shape
    rows, q_cols = queries.shape
    kw = 2 * HD
    kv_here = w_key.shape[1] // HD // H
    e = q_cols // HD
    ex = e + QPK
    nt = n_tok // TOK_SPLIT
    n_units = kv_here * TOK_SPLIT
    f32, bf16 = jnp.float32, jnp.bfloat16
    vmem = pl.BlockSpec(memory_space=pltpu.VMEM)
    hbm = pl.BlockSpec(memory_space=pl.ANY)
    dma = pltpu.SemaphoreType.DMA
    scratch = [
        pltpu.VMEM((n_tok, width), bf16),
        pltpu.VMEM((n_tok, width), bf16),
        pltpu.VMEM((width, 2 * w_key.shape[1]), bf16),
        pltpu.VMEM((rows, q_cols), bf16),
        pltpu.VMEM((H, 1, n_tok), f32),
        pltpu.VMEM((n_tok, HD), f32),
        pltpu.VMEM((n_tok, HD), f32),
        pltpu.VMEM((T, 1, n_tok), jnp.int32),
        pltpu.VMEM((rows, HD), jnp.int32),
        pltpu.VMEM((n_units, X, nt, kw), f32),
        pltpu.VMEM((n_units, X, nt, kw), f32),
        pltpu.VMEM((n_units, X, nt, kw), f32),
        pltpu.VMEM((n_units, X - 1, nt, kw), WIRE),
        pltpu.VMEM((n_units, X - 1, nt, kw), WIRE),
        pltpu.VMEM((T, kv_here, n_tok, kw), bf16),
        pltpu.VMEM((T, ex, rows, n_tok), f32),
        pltpu.VMEM((ex, rows, HD), f32),
        pltpu.VMEM((ex, rows, HD), f32),
        pltpu.VMEM((ex, rows, HD), f32),
        dma((1 + H_PARTS + 2 * H * kv_here,)),
        dma((H,)), dma((H,)),
        dma((T,)), dma((T,)),
        dma((n_units, X)), dma((n_units, X)),
        dma((n_units, X - 1)), dma((n_units, X - 1)),
        dma((2, T - 1, n_units)), dma((2, T - 1, n_units)),
        pltpu.VMEM((rows, QPK * HD), bf16),
        pltpu.VMEM((1, rows), jnp.int32),
        pltpu.VMEM((rows, HD), jnp.int32),
        pltpu.VMEM((QPK, rows, HD), bf16),
        pltpu.VMEM((2, QPK, rows), f32),
        pltpu.VMEM((QPK, rows, HD), bf16),
        pltpu.VMEM((2, QPK, rows), f32),
        dma((4,)), dma((4,)),
        pltpu.VMEM((ex, rows, HD), bf16),
    ]
    return pl.pallas_call(
        functools.partial(kernel, T, H, width * H),
        out_shape=jax.ShapeDtypeStruct((rows, q_cols), bf16),
        in_specs=[hbm, vmem, vmem, hbm, hbm, hbm, vmem],
        out_specs=vmem,
        scratch_shapes=scratch,
        compiler_params=pltpu.CompilerParams(
            collective_id=0, has_side_effects=True, vmem_limit_bytes=60 * 1024 * 1024
        ),
    )(
        hidden, positions, norm_gain.reshape(1, width), w_key, w_value,
        queries, lengths.reshape(1, rows),
    )


def solution(mesh):
    in_specs = (
        P(("groups", "tok"), "head"),
        P(("groups", "tok")),
        P("head"),
        P("head", None),
        P("head", None),
        P(("groups", "tok"), "head"),
        P(("groups", "tok")),
    )
    out_specs = P(("groups", "tok"), "head")
    return jax.shard_map(body, mesh=mesh, in_specs=in_specs, out_specs=out_specs, check_vma=False)
```
